128 devices in a mesh: val: 4 (over x_hi, core), cond: 8 (over z, x_lo), grid: 4 (over y).
Axes of the slice: x: 4 (x_hi: 2, x_lo: 2; x = x_hi * 2 + x_lo), y: 4, z: 4, core: 2. Of those that a mesh axis runs over, the one named last changes fastest.
Arguments:
- valence_orbitals: bfloat16 [16, 96, 9216], P('val', 'grid'), may hold values from -6 to 6
- conduction_orbitals: bfloat16 [32, 96, 9216], P('cond', 'grid'), may hold values from -6 to 6
- valence_energy: float32 [16], replicated, may hold values from -12 to -1
- conduction_energy: float32 [32], replicated, may hold values from 0.5 to 10
- grid_index: int32 [6144], replicated, may hold values from 0 to 884735, as said below
Outputs:
- response: float32 [2, 6144, 6144], P(None, ('val', 'grid'), 'cond')
The draws below stay inside these ranges and needn't reach their ends.
Inputs may be any that keep to these rules, and one draw needn't show every extreme that they name: `grid_index`: distinct flat points of the 96 x 96 x 96 frequency grid.
All inputs are finite; a program needn't handle non-finite values.
Results may differ from the reference program's by a relative error of at most 0.0098.
Values may be sent and summed in bfloat16 or wider, within the bound.
No kernel may reach another device: no remote copies, remote signals or barrier semaphores. Data moves between devices by JAX's collectives and lax.ppermute only.
A program may use at most 128 MiB of HBM per device.

```python
import math
import jax
import jax.numpy as jnp
from jax import lax

NGRID = 96
NG = 6144
NV = 16
NC = 32


def draw_grid_index(key, part):
    point_count = NGRID ** 3
    interior = jax.random.permutation(key, point_count - 2)[:NG - 2] + 1
    return jnp.concatenate([jnp.zeros((1,), jnp.int32), interior.astype(jnp.int32), jnp.full((1,), point_count - 1, jnp.int32)])


def level_of(stream_key, extent, shards, least, high):
    factor_of = 1.0
    for dim, shards_of in shards:
        heights = jax.random.uniform(jax.random.fold_in(jax.random.fold_in(stream_key, 6), dim), (shards_of,), jnp.float32, least / len(shards), high / len(shards))
        factor_of = factor_of * jnp.repeat(jnp.exp(heights), extent[dim] // shards_of).reshape((-1,) + (1,) * (len(extent) - 1 - dim))
    return factor_of


def centred(rng, shape, width, most, shards=(), held_as=jnp.bfloat16):
    result = width * jax.random.normal(rng, shape, jnp.float32)
    if shards:
        result = result * level_of(rng, shape, shards, -0.22, 0.18)
    return jnp.clip(result, -most, most).astype(held_as)


def setup_inputs(seed: int = 0) -> dict:
    key_of = jax.random.split(jax.random.key(seed), 6)
    return {
        "valence_orbitals": centred(key_of[0], (NV, NGRID, NGRID * NGRID), 1.0, 6.0, ((0, 4), (1, 4))),
        "conduction_orbitals": centred(key_of[1], (NC, NGRID, NGRID * NGRID), 1.0, 6.0, ((0, 8), (1, 4))),
        "valence_energy": jnp.clip(jax.random.uniform(key_of[2], (NV,), jnp.float32, -12.0, -1.0), -12.0, -1.0),
        "conduction_energy": jnp.clip(jax.random.uniform(key_of[3], (NC,), jnp.float32, 0.5, 10.0), 0.5, 10.0),
        "grid_index": draw_grid_index(jax.random.fold_in(key_of[5], 71), 0),
    }


freq_squared = 4.0

def line_tables(points):
    indices = jnp.arange(points, dtype=jnp.int32)
    phases = indices[:, None] * indices[None, :] % points
    angles = phases.astype(jnp.float32) * (2.0 * math.pi / points)
    return (jnp.cos(angles).astype(jnp.bfloat16), (-jnp.sin(angles)).astype(jnp.bfloat16))

def reference(valence_orbitals, conduction_orbitals, valence_energy, conduction_energy, grid_index):
    line_cos, line_sin = line_tables(NGRID)
    cos_wide = line_cos.astype(jnp.float32)
    sin_wide = line_sin.astype(jnp.float32)
    z_table = jnp.concatenate([line_cos, line_sin], axis=1)
    scale = NGRID ** (-1.5)

    def one_band(orbital):
        products = (orbital.astype(jnp.float32)[None] * conduction_orbitals.astype(jnp.float32)).astype(jnp.bfloat16)
        flat_rows = products.reshape(NC * NGRID * NGRID, NGRID)
        z_part = jnp.dot(flat_rows, z_table, preferred_element_type=jnp.float32).astype(jnp.bfloat16)
        z_part = z_part.reshape(NC, NGRID, NGRID, 2 * NGRID).astype(jnp.float32)
        first = jnp.einsum('cxyk,yp->cxpk', z_part, cos_wide)
        second = jnp.einsum('cxyk,yp->cxpk', z_part, sin_wide)
        plane_real = first[..., :NGRID] - second[..., NGRID:]
        plane_imag = second[..., :NGRID] + first[..., NGRID:]
        plane = jnp.concatenate([plane_real, plane_imag], axis=-1).astype(jnp.bfloat16).astype(jnp.float32)
        first = jnp.einsum('cxpk,xq->cqpk', plane, cos_wide)
        second = jnp.einsum('cxpk,xq->cqpk', plane, sin_wide)
        full_real = (first[..., :NGRID] - second[..., NGRID:]).reshape(NC, NGRID ** 3)
        full_imag = (second[..., :NGRID] + first[..., NGRID:]).reshape(NC, NGRID ** 3)
        picked_real = jnp.take(full_real, grid_index, axis=1) * scale
        picked_imag = jnp.take(full_imag, grid_index, axis=1) * scale
        return jnp.stack([picked_real, picked_imag]).astype(jnp.bfloat16)
    values = lax.map(one_band, valence_orbitals)
    values = jnp.transpose(values, (1, 0, 2, 3)).reshape(2, NV * NC, NG)
    delta = valence_energy[:, None] - conduction_energy[None, :]
    weights = (4.0 * delta / (delta * delta + freq_squared) / math.sqrt(NV * NC)).reshape(NV * NC)
    scaled = (values.astype(jnp.float32) * weights[None, :, None]).astype(jnp.bfloat16)
    real_sum = jnp.dot(scaled[0].T, values[0], preferred_element_type=jnp.float32) + jnp.dot(scaled[1].T, values[1], preferred_element_type=jnp.float32)
    imag_sum = jnp.dot(scaled[1].T, values[0], preferred_element_type=jnp.float32) - jnp.dot(scaled[0].T, values[1], preferred_element_type=jnp.float32)
    return jnp.stack([real_sum, imag_sum])
```

```python
import math

import jax
import jax.numpy as jnp
import numpy as np
from jax import lax
from jax.experimental import pallas as pl
from jax.experimental.pallas import tpu as pltpu
from jax.sharding import PartitionSpec as P

NGRID = 96
NG = 6144
HALF = NGRID // 2 + 1
PITCH = 52
ROWS = 2 * PITCH
LANES = 128
ENTRY = 6
BLOCK = 128
SUB = 32

freq_squared = 4.0


def line_tables():
    indices = np.arange(NGRID)
    phases = indices[:, None] * indices[None, :] % NGRID
    angles = phases.astype(np.float32) * np.float32(2.0 * math.pi / NGRID)
    cos = np.cos(angles).astype(np.float32).astype(jnp.bfloat16)
    sin = (-np.sin(angles)).astype(np.float32).astype(jnp.bfloat16)
    return cos, sin


def z_matrix(per_group):
    cos, sin = line_tables()
    out = np.zeros((per_group, ROWS, per_group, NGRID), cos.dtype)
    for y in range(per_group):
        out[y, :HALF, y] = cos[:HALF]
        out[y, PITCH : PITCH + HALF, y] = sin[:HALF]
    return out.reshape(per_group * ROWS, per_group * NGRID)


def y_matrix():
    cos, sin = line_tables()
    top = np.concatenate([cos.T, -(sin.T)], axis=1)
    bottom = np.concatenate([sin.T, cos.T], axis=1)
    return np.concatenate([top, bottom], axis=0)


def fold_matrix(tiles):
    out = np.zeros((tiles, SUB, SUB, 8), np.float32)
    for t in range(tiles):
        for j in range(SUB):
            out[t, j, j, t] = 1.0
            out[t, j, j, t + tiles] = 1.0
    return out.reshape(tiles * SUB, SUB * 8).astype(jnp.bfloat16)


def slab_matrix(pairs, depth):
    return np.kron(np.eye(pairs), np.ones((1, depth))).astype(jnp.bfloat16)


def tile_matrix(pairs, depth):
    return np.tile(np.eye(depth), (1, pairs)).astype(jnp.bfloat16)


def spectra_kernel(
    rows_ref, line_ref, val_ref, cond_ref, phase_ref, zmat_ref, ymat_ref, fold_ref, slab_ref,
    tile_ref, out_ref, z_scr, table_scr, phase_scr,
):
    bands_v, depth, points = val_ref.shape
    bands_c = cond_ref.shape[0]
    pairs = bands_v * bands_c
    width = pairs * depth
    tiles = width // LANES
    chunk = zmat_ref.shape[1]
    group_rows = zmat_ref.shape[0]

    wide = [
        jnp.dot(phase_ref[i], tile_ref[...], preferred_element_type=jnp.float32) for i in range(2)
    ]
    zeros = jnp.zeros((NGRID, LANES), jnp.float32)
    for sign in range(2):
        base = sign * NGRID * 16
        for s in range(8):
            t = s % tiles
            lanes = slice(t * LANES, (t + 1) * LANES)
            if s < tiles:
                first, second = wide[0][:, lanes], wide[1][:, lanes]
            elif s < 2 * tiles:
                first, second = -wide[1][:, lanes], wide[0][:, lanes]
            else:
                first, second = zeros, zeros
            if sign:
                second = -second
            phase_scr[pl.ds(base + s, NGRID, stride=16), :] = first
            phase_scr[pl.ds(base + 8 + s, NGRID, stride=16), :] = second
    table_scr[pl.ds(HALF * NGRID * ENTRY, 8), :] = jnp.zeros((8, LANES), jnp.float32)

    def z_step(i, carry):
        at = pl.multiple_of(i * chunk, LANES)
        cond = [cond_ref[c, :, pl.ds(at, chunk)].astype(jnp.float32) for c in range(bands_c)]
        parts = []
        for v in range(bands_v):
            orbital = val_ref[v, :, pl.ds(at, chunk)].astype(jnp.float32)
            parts += [orbital * cond[c] for c in range(bands_c)]
        products = jnp.concatenate(parts, axis=0).astype(jnp.bfloat16)
        z_part = lax.dot_general(
            zmat_ref[...], products, (((1,), (1,)), ((), ())), preferred_element_type=jnp.float32
        )
        row = pl.multiple_of(i * group_rows, 8)
        for t in range(tiles):
            z_scr[t, pl.ds(row, group_rows), :] = z_part[:, t * LANES : (t + 1) * LANES]
        return carry

    lax.fori_loop(0, points // chunk, z_step, 0)

    def y_step(q, carry):
        z_part = jnp.concatenate(
            [
                jnp.concatenate(
                    [
                        z_scr[t, pl.ds(q + part * PITCH, NGRID, stride=ROWS), :]
                        for t in range(tiles)
                    ],
                    axis=1,
                )
                for part in range(2)
            ],
            axis=0,
        ).astype(jnp.bfloat16)
        plane = jnp.dot(ymat_ref[...], z_part, preferred_element_type=jnp.float32)
        for part in range(2):
            for t in range(tiles):
                table_scr[pl.ds(q * (NGRID * ENTRY) + part * tiles + t, NGRID, stride=ENTRY), :] = (
                    plane[part * NGRID : (part + 1) * NGRID, t * LANES : (t + 1) * LANES]
                )
        return carry

    lax.fori_loop(0, HALF, y_step, 0)

    scale = NGRID ** (-1.5)

    def pick_step(i, carry):
        first = i * BLOCK
        picked = []
        for sub in range(BLOCK // SUB):
            real, imag = [], []
            for j in range(SUB):
                at = first + sub * SUB + j
                entry = table_scr[pl.ds(rows_ref[at], 8), :]
                line = pl.multiple_of(line_ref[at], 16)
                real.append(entry * phase_scr[pl.ds(line, 8), :])
                imag.append(entry * phase_scr[pl.ds(line + 8, 8), :])
            terms = jnp.concatenate(
                [jnp.concatenate(real, axis=0), jnp.concatenate(imag, axis=0)], axis=1
            ).astype(jnp.bfloat16)
            folded = jnp.dot(fold_ref[...], terms, preferred_element_type=jnp.float32)
            picked.append(
                [
                    jnp.concatenate(
                        [
                            folded[t * SUB : (t + 1) * SUB, part * LANES : (part + 1) * LANES]
                            for t in range(tiles)
                        ],
                        axis=1,
                    )
                    for part in range(2)
                ]
            )
        at = pl.multiple_of(first, BLOCK)
        for part in range(2):
            lines = jnp.concatenate([p[part] for p in picked], axis=0).astype(jnp.bfloat16)
            value = lax.dot_general(
                slab_ref[...], lines, (((1,), (1,)), ((), ())), preferred_element_type=jnp.float32
            )
            out_ref[part, :, pl.ds(at, BLOCK)] = (value * scale).astype(out_ref.dtype)
        return carry

    lax.fori_loop(0, out_ref.shape[2] // BLOCK, pick_step, 0)


def picked_partials(valence_orbitals, conduction_orbitals, grid_index, slab):
    bands_v, depth, points = valence_orbitals.shape
    bands_c = conduction_orbitals.shape[0]
    pairs = bands_v * bands_c
    tiles = pairs * depth // LANES
    cos, sin = line_tables()
    phases = lax.dynamic_slice_in_dim(
        jnp.asarray(np.stack([cos.T, sin.T])), slab * depth, depth, 2
    )
    plane_size = NGRID * NGRID
    k = grid_index // plane_size
    p = grid_index // NGRID % NGRID
    q = grid_index % NGRID
    mirrored = q >= HALF
    k = jnp.where(mirrored, (NGRID - k) % NGRID, k)
    p = jnp.where(mirrored, (NGRID - p) % NGRID, p)
    q = jnp.where(mirrored, NGRID - q, q)
    rows = (q * NGRID + p) * ENTRY
    lines = (k + jnp.where(mirrored, NGRID, 0)) * 16
    constants = [
        jnp.asarray(a)
        for a in (
            z_matrix(4), y_matrix(), fold_matrix(tiles), slab_matrix(pairs, depth),
            tile_matrix(pairs, depth),
        )
    ]
    smem = pl.BlockSpec(memory_space=pltpu.SMEM)
    vmem = pl.BlockSpec(memory_space=pltpu.VMEM)
    return pl.pallas_call(
        spectra_kernel,
        out_shape=jax.ShapeDtypeStruct((2, pairs, NG), jnp.bfloat16),
        in_specs=[smem, smem] + [vmem] * (3 + len(constants)),
        out_specs=vmem,
        scratch_shapes=[
            pltpu.VMEM((tiles, NGRID * ROWS, LANES), jnp.float32),
            pltpu.VMEM((HALF * NGRID * ENTRY + 8, LANES), jnp.float32),
            pltpu.VMEM((2 * NGRID * 16, LANES), jnp.float32),
        ],
        name="spectra",
    )(rows, lines, valence_orbitals, conduction_orbitals, phases, *constants)


def local(valence_orbitals, conduction_orbitals, valence_energy, conduction_energy, grid_index):
    valence_groups = lax.axis_size("val")
    conduction_groups = lax.axis_size("cond")
    grid_groups = lax.axis_size("grid")
    valence_local = valence_orbitals.shape[0]
    conduction_local = conduction_orbitals.shape[0]
    pair_count = valence_local * conduction_local
    partial_values = picked_partials(
        valence_orbitals, conduction_orbitals, grid_index, lax.axis_index("grid")
    )
    pair_values = lax.psum(partial_values, "grid")
    delta = valence_energy[:, None] - conduction_energy[None, :]
    all_pairs = valence_energy.shape[0] * conduction_energy.shape[0]
    weights = 4.0 * delta / (delta * delta + freq_squared) / math.sqrt(all_pairs)
    weights = weights.reshape(valence_groups, valence_local, conduction_groups, conduction_local)
    weights = jnp.transpose(weights, (0, 2, 1, 3)).reshape(all_pairs)
    row_width = NG // (valence_groups * grid_groups)
    split_view = pair_values.reshape(2, pair_count, valence_groups, grid_groups, row_width)
    grid_rows = lax.dynamic_index_in_dim(split_view, lax.axis_index("grid"), 3, keepdims=False)
    everything = lax.all_gather(
        grid_rows.reshape(2, pair_count, valence_groups * row_width),
        ("val", "cond"),
        axis=1,
        tiled=True,
    )
    row_values = lax.dynamic_slice_in_dim(
        everything, lax.axis_index("val") * row_width, row_width, 2
    )
    scaled_rows = (row_values.astype(jnp.float32) * weights[None, :, None]).astype(jnp.bfloat16)
    by_column = lax.all_to_all(pair_values, "cond", split_axis=2, concat_axis=1, tiled=True)
    contract = (((0,), (0,)), ((), ()))
    piece = lax.all_gather(by_column, "val", axis=1, tiled=True)
    real_sum = lax.dot_general(
        scaled_rows[0], piece[0], contract, preferred_element_type=jnp.float32
    )
    real_sum = real_sum + lax.dot_general(
        scaled_rows[1], piece[1], contract, preferred_element_type=jnp.float32
    )
    imag_sum = lax.dot_general(
        scaled_rows[1], piece[0], contract, preferred_element_type=jnp.float32
    )
    imag_sum = imag_sum - lax.dot_general(
        scaled_rows[0], piece[1], contract, preferred_element_type=jnp.float32
    )
    return jnp.stack([real_sum, imag_sum])


def solution(mesh):
    return jax.shard_map(
        local,
        mesh=mesh,
        in_specs=(P("val", "grid", None), P("cond", "grid", None), P(), P(), P()),
        out_specs=P(None, ("val", "grid"), "cond"),
        check_vma=False,
    )
```

```python
import math

import jax
import jax.numpy as jnp
import numpy as np
from jax import lax
from jax.experimental import pallas as pl
from jax.experimental.pallas import tpu as pltpu
from jax.sharding import PartitionSpec as P

NGRID = 96
NG = 6144
HALF = NGRID // 2 + 1
PITCH = 52
ROWS = 2 * PITCH
LANES = 128
ENTRY = 6
BLOCK = 128
SUB = 32

freq_squared = 4.0


def line_tables():
    indices = np.arange(NGRID)
    phases = indices[:, None] * indices[None, :] % NGRID
    angles = phases.astype(np.float32) * np.float32(2.0 * math.pi / NGRID)
    cos = np.cos(angles).astype(np.float32).astype(jnp.bfloat16)
    sin = (-np.sin(angles)).astype(np.float32).astype(jnp.bfloat16)
    return cos, sin


def z_matrix(per_group):
    cos, sin = line_tables()
    out = np.zeros((per_group, ROWS, per_group, NGRID), cos.dtype)
    for y in range(per_group):
        out[y, :HALF, y] = cos[:HALF]
        out[y, PITCH : PITCH + HALF, y] = sin[:HALF]
    return out.reshape(per_group * ROWS, per_group * NGRID)


def y_matrix():
    cos, sin = line_tables()
    top = np.concatenate([cos.T, -(sin.T)], axis=1)
    bottom = np.concatenate([sin.T, cos.T], axis=1)
    return np.concatenate([top, bottom], axis=0)


def fold_matrix(tiles):
    out = np.zeros((tiles, SUB, SUB, 8), np.float32)
    for t in range(tiles):
        for j in range(SUB):
            out[t, j, j, t] = 1.0
            out[t, j, j, t + tiles] = 1.0
    return out.reshape(tiles * SUB, SUB * 8).astype(jnp.bfloat16)


def slab_matrix(pairs, depth):
    return np.kron(np.eye(pairs), np.ones((1, depth))).astype(jnp.bfloat16)


def tile_matrix(pairs, depth):
    return np.tile(np.eye(depth), (1, pairs)).astype(jnp.bfloat16)


def spectra_kernel(
    rows_ref, line_ref, val_ref, cond_ref, phase_ref, zmat_ref, ymat_ref, fold_ref, slab_ref,
    tile_ref, row_out, col_out, z_scr, table_scr, phase_scr,
):
    bands_v, depth, points = val_ref.shape
    bands_c = cond_ref.shape[0]
    pairs = bands_v * bands_c
    width = pairs * depth
    tiles = width // LANES
    chunk = zmat_ref.shape[1]
    group_rows = zmat_ref.shape[0]

    wide = [
        jnp.dot(phase_ref[i], tile_ref[...], preferred_element_type=jnp.float32) for i in range(2)
    ]
    zeros = jnp.zeros((NGRID, LANES), jnp.float32)
    for sign in range(2):
        base = sign * NGRID * 16
        for s in range(8):
            t = s % tiles
            lanes = slice(t * LANES, (t + 1) * LANES)
            if s < tiles:
                first, second = wide[0][:, lanes], wide[1][:, lanes]
            elif s < 2 * tiles:
                first, second = -wide[1][:, lanes], wide[0][:, lanes]
            else:
                first, second = zeros, zeros
            if sign:
                second = -second
            phase_scr[pl.ds(base + s, NGRID, stride=16), :] = first
            phase_scr[pl.ds(base + 8 + s, NGRID, stride=16), :] = second
    table_scr[pl.ds(HALF * NGRID * ENTRY, 8), :] = jnp.zeros((8, LANES), jnp.float32)

    def z_step(i, carry):
        at = pl.multiple_of(i * chunk, LANES)
        cond = [cond_ref[c, :, pl.ds(at, chunk)].astype(jnp.float32) for c in range(bands_c)]
        parts = []
        for v in range(bands_v):
            orbital = val_ref[v, :, pl.ds(at, chunk)].astype(jnp.float32)
            parts += [orbital * cond[c] for c in range(bands_c)]
        products = jnp.concatenate(parts, axis=0).astype(jnp.bfloat16)
        z_part = lax.dot_general(
            zmat_ref[...], products, (((1,), (1,)), ((), ())), preferred_element_type=jnp.float32
        )
        row = pl.multiple_of(i * group_rows, 8)
        for t in range(tiles):
            z_scr[t, pl.ds(row, group_rows), :] = z_part[:, t * LANES : (t + 1) * LANES]
        return carry

    lax.fori_loop(0, points // chunk, z_step, 0)

    def y_step(q, carry):
        z_part = jnp.concatenate(
            [
                jnp.concatenate(
                    [
                        z_scr[t, pl.ds(q + part * PITCH, NGRID, stride=ROWS), :]
                        for t in range(tiles)
                    ],
                    axis=1,
                )
                for part in range(2)
            ],
            axis=0,
        ).astype(jnp.bfloat16)
        plane = jnp.dot(ymat_ref[...], z_part, preferred_element_type=jnp.float32)
        for part in range(2):
            for t in range(tiles):
                table_scr[pl.ds(q * (NGRID * ENTRY) + part * tiles + t, NGRID, stride=ENTRY), :] = (
                    plane[part * NGRID : (part + 1) * NGRID, t * LANES : (t + 1) * LANES]
                )
        return carry

    lax.fori_loop(0, HALF, y_step, 0)

    scale = NGRID ** (-1.5)

    def pick_step(i, carry):
        first = i * BLOCK
        picked = []
        for sub in range(BLOCK // SUB):
            real, imag = [], []
            for j in range(SUB):
                at = first + sub * SUB + j
                entry = table_scr[pl.ds(rows_ref[at], 8), :]
                line = pl.multiple_of(line_ref[at], 16)
                real.append(entry * phase_scr[pl.ds(line, 8), :])
                imag.append(entry * phase_scr[pl.ds(line + 8, 8), :])
            terms = jnp.concatenate(
                [jnp.concatenate(real, axis=0), jnp.concatenate(imag, axis=0)], axis=1
            ).astype(jnp.bfloat16)
            folded = jnp.dot(fold_ref[...], terms, preferred_element_type=jnp.float32)
            picked.append(
                [
                    jnp.concatenate(
                        [
                            folded[t * SUB : (t + 1) * SUB, part * LANES : (part + 1) * LANES]
                            for t in range(tiles)
                        ],
                        axis=1,
                    )
                    for part in range(2)
                ]
            )
        row_block = first // row_out.shape[3]
        row_at = pl.multiple_of(first % row_out.shape[3], BLOCK)
        col_at = pl.multiple_of(first % col_out.shape[3], BLOCK)
        slabs, piece = col_out.shape[1:3]
        for part in range(2):
            lines = jnp.concatenate([p[part] for p in picked], axis=0).astype(jnp.bfloat16)
            value = lax.dot_general(
                slab_ref[...], lines, (((1,), (1,)), ((), ())), preferred_element_type=jnp.float32
            )
            value = value * scale
            row_out[
                row_block % slabs, row_block // slabs, part * pairs : (part + 1) * pairs,
                pl.ds(row_at, BLOCK),
            ] = value.astype(row_out.dtype)
            for h in range(pairs // piece):
                col_out[
                    first // col_out.shape[3], part * (pairs // piece) + h, :, pl.ds(col_at, BLOCK)
                ] = value[h * piece : (h + 1) * piece].astype(col_out.dtype)
        return carry

    lax.fori_loop(0, NG // BLOCK, pick_step, 0)


def picked_partials(valence_orbitals, conduction_orbitals, grid_index, slab, groups):
    val_groups, cond_groups, slabs = groups
    bands_v, depth, points = valence_orbitals.shape
    bands_c = conduction_orbitals.shape[0]
    pairs = bands_v * bands_c
    tiles = pairs * depth // LANES
    cos, sin = line_tables()
    phases = lax.dynamic_slice_in_dim(
        jnp.asarray(np.stack([cos.T, sin.T])), slab * depth, depth, 2
    )
    plane_size = NGRID * NGRID
    k = grid_index // plane_size
    p = grid_index // NGRID % NGRID
    q = grid_index % NGRID
    mirrored = q >= HALF
    k = jnp.where(mirrored, (NGRID - k) % NGRID, k)
    p = jnp.where(mirrored, (NGRID - p) % NGRID, p)
    q = jnp.where(mirrored, NGRID - q, q)
    rows = (q * NGRID + p) * ENTRY
    lines = (k + jnp.where(mirrored, NGRID, 0)) * 16
    constants = [
        jnp.asarray(a)
        for a in (
            z_matrix(4), y_matrix(), fold_matrix(tiles), slab_matrix(pairs, depth),
            tile_matrix(pairs, depth),
        )
    ]
    smem = pl.BlockSpec(memory_space=pltpu.SMEM)
    vmem = pl.BlockSpec(memory_space=pltpu.VMEM)
    return pl.pallas_call(
        spectra_kernel,
        out_shape=[
            jax.ShapeDtypeStruct(
                (slabs, val_groups, 2 * pairs, NG // (val_groups * slabs)), jnp.bfloat16
            ),
            jax.ShapeDtypeStruct(
                (cond_groups, slabs, 2 * pairs // slabs, NG // cond_groups), jnp.bfloat16
            ),
        ],
        in_specs=[smem, smem] + [vmem] * (3 + len(constants)),
        out_specs=[vmem, vmem],
        scratch_shapes=[
            pltpu.VMEM((tiles, NGRID * ROWS, LANES), jnp.float32),
            pltpu.VMEM((HALF * NGRID * ENTRY + 8, LANES), jnp.float32),
            pltpu.VMEM((2 * NGRID * 16, LANES), jnp.float32),
        ],
        name="spectra",
    )(rows, lines, valence_orbitals, conduction_orbitals, phases, *constants)


def swap(value, axis, partner, first):
    count = lax.axis_size(axis)
    other = lax.ppermute(value, axis, [(i, partner(i)) for i in range(count)])
    return jnp.where(
        first, jnp.concatenate([value, other], 0), jnp.concatenate([other, value], 0)
    )


def row_values(partials):
    v, c, g = (lax.axis_index(name) for name in ("val", "cond", "grid"))
    slabs, groups, lines, width = partials.shape
    total = lax.dynamic_index_in_dim(partials, g, 0, keepdims=False).astype(jnp.float32)
    for step in range(1, slabs):
        piece = lax.dynamic_index_in_dim(partials, (g + step) % slabs, 0, keepdims=False)
        ring = [(i, (i + step) % slabs) for i in range(slabs)]
        total = total + lax.ppermute(piece, "grid", ring).astype(jnp.float32)
    total = total.astype(jnp.bfloat16)
    pieces = [lax.dynamic_index_in_dim(total, v, 0, keepdims=False)]
    for bits in range(1, groups):
        piece = lax.dynamic_index_in_dim(total, v ^ bits, 0, keepdims=False)
        pieces.append(lax.ppermute(piece, "val", [(i, i ^ bits) for i in range(groups)]))
    value = jnp.stack(pieces).reshape(2, 2, lines, width)
    value = jnp.where(v % 2 == 0, value, value[:, ::-1])
    value = jnp.where(v // 2 == 0, value, value[::-1])
    value = value.reshape(1, groups, lines, width)
    value = swap(value, "cond", lambda i: i ^ 1, c % 2 == 0)
    value = swap(value, "cond", lambda i: i ^ 2, c // 2 % 2 == 0)
    return swap(value, "cond", lambda i: (3 - i // 2) * 2 + i % 2, c // 4 == 0)


def column_values(partials):
    v, g = lax.axis_index("val"), lax.axis_index("grid")
    groups, slabs, piece, width = partials.shape
    received = lax.all_to_all(
        partials.reshape(groups * slabs, piece, width), ("cond", "grid"), 0, 0, tiled=True
    )
    value = jnp.sum(received.reshape(groups, slabs, piece, width).astype(jnp.float32), 1)
    value = value.astype(jnp.bfloat16).reshape(1, groups * piece, width)
    value = swap(value, "val", lambda i: i ^ 2, v // 2 == 0)
    value = swap(value, "grid", lambda i: i ^ 1, g % 2 == 0)
    value = swap(value, "grid", lambda i: 3 - i, g // 2 == 0)
    value = swap(value, "val", lambda i: i ^ 1, v % 2 == 0)
    return value.reshape(-1, width)


def row_order(value):
    return jnp.transpose(value, (2, 3, 1, 0, 4, 5))


def local(valence_orbitals, conduction_orbitals, valence_energy, conduction_energy, grid_index):
    groups = tuple(lax.axis_size(name) for name in ("val", "cond", "grid"))
    val_groups, cond_groups, slabs = groups
    valence_local = valence_orbitals.shape[0]
    conduction_local = conduction_orbitals.shape[0]
    row_partials, column_partials = picked_partials(
        valence_orbitals, conduction_orbitals, grid_index, lax.axis_index("grid"), groups
    )
    rows = row_values(row_partials)
    columns = column_values(column_partials)
    delta = valence_energy[:, None] - conduction_energy[None, :]
    all_pairs = valence_energy.shape[0] * conduction_energy.shape[0]
    weights = 4.0 * delta / (delta * delta + freq_squared) / math.sqrt(all_pairs)
    weights = weights.reshape(val_groups, valence_local, cond_groups, conduction_local)
    weights = jnp.transpose(weights, (2, 0, 1, 3)).reshape(cond_groups, val_groups, 1, -1)
    weights = jnp.concatenate([weights, weights], axis=2)
    width = rows.shape[-1]
    split = (cond_groups, 2, val_groups // 2, slabs, rows.shape[2] // slabs)
    scaled = rows.reshape(split + (width,)).astype(jnp.float32) * weights.reshape(split + (1,))
    scaled = row_order(scaled.astype(jnp.bfloat16))
    swapped = jnp.concatenate([scaled[:, slabs // 2 :], -scaled[:, : slabs // 2]], axis=1)
    left = jnp.concatenate(
        [scaled.reshape(2 * all_pairs, width), swapped.reshape(2 * all_pairs, width)], axis=1
    )
    response = lax.dot_general(
        left, columns, (((0,), (0,)), ((), ())), preferred_element_type=jnp.float32
    )
    return response.reshape(2, width, columns.shape[1])


def solution(mesh):
    return jax.shard_map(
        local,
        mesh=mesh,
        in_specs=(P("val", "grid", None), P("cond", "grid", None), P(), P(), P()),
        out_specs=P(None, ("val", "grid"), "cond"),
        check_vma=False,
    )
```

```python
import math

import jax
import jax.numpy as jnp
import numpy as np
from jax import lax
from jax.experimental import pallas as pl
from jax.experimental.pallas import tpu as pltpu
from jax.sharding import PartitionSpec as P

NGRID = 96
NG = 6144
HALF = NGRID // 2 + 1
PITCH = 52
ROWS = 2 * PITCH
LANES = 128
ENTRY = 6
BLOCK = 128
GROUP = 4
FREQS = HALF + 1
YPAIRS = 5
FETCH = 4
SUB = 32

freq_squared = 4.0


def line_tables():
    indices = np.arange(NGRID)
    phases = indices[:, None] * indices[None, :] % NGRID
    angles = phases.astype(np.float32) * np.float32(2.0 * math.pi / NGRID)
    cos = np.cos(angles).astype(np.float32).astype(jnp.bfloat16)
    sin = (-np.sin(angles)).astype(np.float32).astype(jnp.bfloat16)
    return cos, sin


def z_matrix():
    cos, sin = line_tables()
    out = np.zeros((GROUP, ROWS, GROUP, NGRID), cos.dtype)
    for y in range(GROUP):
        out[y, :HALF, y] = cos[:HALF]
        out[y, PITCH : PITCH + HALF, y] = sin[:HALF]
    return out.reshape(GROUP * ROWS, GROUP * NGRID)


def y_matrix():
    cos, sin = line_tables()
    top = np.concatenate([cos.T, -(sin.T)], axis=1)
    bottom = np.concatenate([sin.T, cos.T], axis=1)
    return np.concatenate([top, bottom], axis=0)


def fold_matrix(tiles):
    out = np.zeros((tiles, SUB, SUB, 8), np.float32)
    for t in range(tiles):
        for j in range(SUB):
            out[t, j, j, t] = 1.0
            out[t, j, j, t + tiles] = 1.0
    return out.reshape(tiles * SUB, SUB * 8).astype(jnp.bfloat16)


def slab_matrix(pairs, depth):
    return np.kron(np.eye(pairs), np.ones((1, depth))).astype(jnp.bfloat16)


def tile_matrix(pairs, depth):
    return np.tile(np.eye(depth), (1, pairs)).astype(jnp.bfloat16)


def spectra_kernel(
    index_ref, val_ref, cond_ref, phase_ref, zmat_ref, ymat_ref, fold_ref, slab_ref,
    tile_ref, row_out, col_out, z_scr, table_scr, phase_scr, prod_a, prod_b, lines_a, lines_b,
    index_a, index_b, index_sem,
):
    index_scr = (index_a, index_b)
    bands_v, depth, points = val_ref.shape
    bands_c = cond_ref.shape[0]
    pairs = bands_v * bands_c
    width = pairs * depth
    tiles = width // LANES
    chunk = GROUP * NGRID

    def fetch(block, slot):
        pltpu.make_async_copy(
            index_ref.at[pl.ds(block * FETCH, FETCH)], index_scr[slot], index_sem.at[slot]
        ).start()

    fetch(0, 0)
    fetch(1, 1)

    wide = [
        jnp.dot(phase_ref[i], tile_ref[...], preferred_element_type=jnp.float32) for i in range(2)
    ]
    zeros = jnp.zeros((NGRID, LANES), jnp.float32)
    for sign in range(2):
        base = sign * NGRID * 16
        for s in range(8):
            t = s % tiles
            lanes = slice(t * LANES, (t + 1) * LANES)
            if s < tiles:
                first, second = wide[0][:, lanes], wide[1][:, lanes]
            elif s < 2 * tiles:
                first, second = -wide[1][:, lanes], wide[0][:, lanes]
            else:
                first, second = zeros, zeros
            if sign:
                second = -second
            phase_scr[pl.ds(base + s, NGRID, stride=16), :] = first
            phase_scr[pl.ds(base + 8 + s, NGRID, stride=16), :] = second
    table_scr[pl.ds(FREQS * NGRID * ENTRY, 8), :] = jnp.zeros((8, LANES), jnp.float32)

    def multiply(i, prod):
        for half in range(2):
            at = pl.multiple_of((2 * i + half) * chunk, LANES)
            cond = [cond_ref[c, :, pl.ds(at, chunk)].astype(jnp.float32) for c in range(bands_c)]
            for v in range(bands_v):
                orbital = val_ref[v, :, pl.ds(at, chunk)].astype(jnp.float32)
                rows = jnp.concatenate([orbital * cond[c] for c in range(bands_c)], axis=0)
                first = half * width + v * bands_c * depth
                prod[first : first + bands_c * depth, :] = rows.astype(jnp.bfloat16)

    def z_transform(i, prod):
        for y0, y1, k0, k1 in ((0, 2, 0, 256), (2, 3, 0, 384), (3, 4, 256, 384)):
            z_part = lax.dot_general(
                zmat_ref[y0 * ROWS : y1 * ROWS, k0:k1], prod[:, k0:k1],
                (((1,), (1,)), ((), ())), preferred_element_type=jnp.float32,
            )
            for half in range(2):
                row = pl.multiple_of(((2 * i + half) * GROUP + y0) * ROWS, 8)
                for t in range(tiles):
                    lane = half * width + t * LANES
                    z_scr[t, pl.ds(row, (y1 - y0) * ROWS), :] = z_part[:, lane : lane + LANES]

    z_last = points // (2 * chunk) - 1
    multiply(0, prod_a)

    def z_step(i, carry):
        z_transform(2 * i, prod_a)
        multiply(2 * i + 1, prod_b)
        z_transform(2 * i + 1, prod_b)
        multiply(jnp.minimum(2 * i + 2, z_last), prod_a)
        return carry

    lax.fori_loop(0, (z_last + 1) // 2, z_step, 0)

    def y_step(i, carry):
        for pair in range(YPAIRS):
            first = (i * YPAIRS + pair) * 2
            z_part = jnp.concatenate(
                [
                    jnp.concatenate(
                        [
                            z_scr[t, pl.ds(first + q + part * PITCH, NGRID, stride=ROWS), :]
                            for q in range(2)
                            for t in range(tiles)
                        ],
                        axis=1,
                    )
                    for part in range(2)
                ],
                axis=0,
            ).astype(jnp.bfloat16)
            plane = jnp.dot(ymat_ref[...], z_part, preferred_element_type=jnp.float32)
            for q in range(2):
                for part in range(2):
                    for t in range(tiles):
                        at = (first + q) * (NGRID * ENTRY) + part * tiles + t
                        lane = (q * tiles + t) * LANES
                        table_scr[pl.ds(at, NGRID, stride=ENTRY), :] = plane[
                            part * NGRID : (part + 1) * NGRID, lane : lane + LANES
                        ]
        return carry

    lax.fori_loop(0, FREQS // (2 * YPAIRS), y_step, 0)

    scale = NGRID ** (-1.5)

    def gather(slot, row, lines):
        for sub in range(BLOCK // SUB):
            real, imag = [], []
            for j in range(sub * SUB, (sub + 1) * SUB):
                entry = table_scr[pl.ds(index_scr[slot][row, 0, j], 8), :]
                line = pl.multiple_of(index_scr[slot][row, 1, j], 16)
                real.append(entry * phase_scr[pl.ds(line, 8), :])
                imag.append(entry * phase_scr[pl.ds(line + 8, 8), :])
            terms = jnp.concatenate(
                [jnp.concatenate(real, axis=0), jnp.concatenate(imag, axis=0)], axis=1
            ).astype(jnp.bfloat16)
            folded = jnp.dot(fold_ref[...], terms, preferred_element_type=jnp.float32)
            folded = folded.astype(jnp.bfloat16)
            for part in range(2):
                for t in range(tiles):
                    first = part * BLOCK + sub * SUB
                    lines[first : first + SUB, t * LANES : (t + 1) * LANES] = folded[
                        t * SUB : (t + 1) * SUB, part * LANES : (part + 1) * LANES
                    ]

    def add_x(block, lines):
        first = block * BLOCK
        row_block = first // row_out.shape[3]
        row_at = pl.multiple_of(first % row_out.shape[3], BLOCK)
        col_at = pl.multiple_of(first % col_out.shape[3], BLOCK)
        slabs, piece = col_out.shape[1:3]
        both = lax.dot_general(
            slab_ref[...], lines[...], (((1,), (1,)), ((), ())), preferred_element_type=jnp.float32
        )
        both = both * scale
        for part in range(2):
            value = both[:, part * BLOCK : (part + 1) * BLOCK]
            row_out[
                row_block % slabs, row_block // slabs, part * pairs : (part + 1) * pairs,
                pl.ds(row_at, BLOCK),
            ] = value.astype(row_out.dtype)
            for h in range(pairs // piece):
                col_out[
                    first // col_out.shape[3], part * (pairs // piece) + h, :, pl.ds(col_at, BLOCK)
                ] = value[h * piece : (h + 1) * piece].astype(col_out.dtype)

    def await_fetch(slot):
        pltpu.make_async_copy(
            index_ref.at[pl.ds(0, FETCH)], index_scr[slot], index_sem.at[slot]
        ).wait()

    last = NG // (BLOCK * FETCH) - 1
    await_fetch(0)
    gather(0, 0, lines_a)
    buffers = (lines_a, lines_b)

    def pick_step(i, carry):
        for n in range(2 * FETCH):
            slot, row = (n + 1) // FETCH % 2, (n + 1) % FETCH
            if row == 0:
                fetch(jnp.minimum(2 * i + n // FETCH + 2, last), 1 - slot)
                await_fetch(slot)
            gather(slot, row, buffers[(n + 1) % 2])
            add_x(2 * FETCH * i + n, buffers[n % 2])
        return carry

    lax.fori_loop(0, (last + 1) // 2, pick_step, 0)
    await_fetch(1)


def picked_partials(valence_orbitals, conduction_orbitals, grid_index, slab, groups):
    val_groups, cond_groups, slabs = groups
    bands_v, depth, points = valence_orbitals.shape
    bands_c = conduction_orbitals.shape[0]
    pairs = bands_v * bands_c
    tiles = pairs * depth // LANES
    cos, sin = line_tables()
    phases = lax.dynamic_slice_in_dim(
        jnp.asarray(np.stack([cos.T, sin.T])), slab * depth, depth, 2
    )
    plane_size = NGRID * NGRID
    k = grid_index // plane_size
    p = grid_index // NGRID % NGRID
    q = grid_index % NGRID
    mirrored = q >= HALF
    k = jnp.where(mirrored, (NGRID - k) % NGRID, k)
    p = jnp.where(mirrored, (NGRID - p) % NGRID, p)
    q = jnp.where(mirrored, NGRID - q, q)
    rows = (q * NGRID + p) * ENTRY
    lines = (k + jnp.where(mirrored, NGRID, 0)) * 16
    constants = [
        jnp.asarray(a)
        for a in (
            z_matrix(), y_matrix(), fold_matrix(tiles), slab_matrix(pairs, depth),
            tile_matrix(pairs, depth),
        )
    ]
    index = jnp.stack([rows.reshape(-1, BLOCK), lines.reshape(-1, BLOCK)], axis=1)
    vmem = pl.BlockSpec(memory_space=pltpu.VMEM)
    return pl.pallas_call(
        spectra_kernel,
        out_shape=[
            jax.ShapeDtypeStruct(
                (slabs, val_groups, 2 * pairs, NG // (val_groups * slabs)), jnp.bfloat16
            ),
            jax.ShapeDtypeStruct(
                (cond_groups, slabs, 2 * pairs // slabs, NG // cond_groups), jnp.bfloat16
            ),
        ],
        in_specs=[pl.BlockSpec(memory_space=pl.ANY)] + [vmem] * (3 + len(constants)),
        out_specs=[vmem, vmem],
        scratch_shapes=[
            pltpu.VMEM((tiles, NGRID * ROWS, LANES), jnp.float32),
            pltpu.VMEM((FREQS * NGRID * ENTRY + 8, LANES), jnp.float32),
            pltpu.VMEM((2 * NGRID * 16, LANES), jnp.float32),
            pltpu.VMEM((2 * pairs * depth, GROUP * NGRID), jnp.bfloat16),
            pltpu.VMEM((2 * pairs * depth, GROUP * NGRID), jnp.bfloat16),
            pltpu.VMEM((2 * BLOCK, pairs * depth), jnp.bfloat16),
            pltpu.VMEM((2 * BLOCK, pairs * depth), jnp.bfloat16),
            pltpu.SMEM((FETCH, 2, BLOCK), jnp.int32),
            pltpu.SMEM((FETCH, 2, BLOCK), jnp.int32),
            pltpu.SemaphoreType.DMA((2,)),
        ],
        name="spectra",
    )(index, valence_orbitals, conduction_orbitals, phases, *constants)


def swap(value, axis, partner, first):
    count = lax.axis_size(axis)
    other = lax.ppermute(value, axis, [(i, partner(i)) for i in range(count)])
    return jnp.where(
        first, jnp.concatenate([value, other], 0), jnp.concatenate([other, value], 0)
    )


def row_values(partials):
    v, c, g = (lax.axis_index(name) for name in ("val", "cond", "grid"))
    slabs, groups, lines, width = partials.shape
    total = lax.dynamic_index_in_dim(partials, g, 0, keepdims=False).astype(jnp.float32)
    for step in range(1, slabs):
        piece = lax.dynamic_index_in_dim(partials, (g + step) % slabs, 0, keepdims=False)
        ring = [(i, (i + step) % slabs) for i in range(slabs)]
        total = total + lax.ppermute(piece, "grid", ring).astype(jnp.float32)
    total = total.astype(jnp.bfloat16)
    pieces = [lax.dynamic_index_in_dim(total, v, 0, keepdims=False)]
    for bits in range(1, groups):
        piece = lax.dynamic_index_in_dim(total, v ^ bits, 0, keepdims=False)
        pieces.append(lax.ppermute(piece, "val", [(i, i ^ bits) for i in range(groups)]))
    value = jnp.stack(pieces).reshape(2, 2, lines, width)
    value = jnp.where(v % 2 == 0, value, value[:, ::-1])
    value = jnp.where(v // 2 == 0, value, value[::-1])
    value = value.reshape(1, groups, lines, width)
    value = swap(value, "cond", lambda i: i ^ 1, c % 2 == 0)
    value = swap(value, "cond", lambda i: i ^ 2, c // 2 % 2 == 0)
    return swap(value, "cond", lambda i: (3 - i // 2) * 2 + i % 2, c // 4 == 0)


def column_values(partials):
    v, g = lax.axis_index("val"), lax.axis_index("grid")
    groups, slabs, piece, width = partials.shape
    received = lax.all_to_all(
        partials.reshape(groups * slabs, piece, width), ("cond", "grid"), 0, 0, tiled=True
    )
    value = jnp.sum(received.reshape(groups, slabs, piece, width).astype(jnp.float32), 1)
    value = value.astype(jnp.bfloat16).reshape(1, groups * piece, width)
    value = swap(value, "val", lambda i: i ^ 2, v // 2 == 0)
    value = swap(value, "grid", lambda i: i ^ 1, g % 2 == 0)
    value = swap(value, "grid", lambda i: 3 - i, g // 2 == 0)
    value = swap(value, "val", lambda i: i ^ 1, v % 2 == 0)
    return value.reshape(-1, width)


def row_order(value):
    return jnp.transpose(value, (2, 3, 1, 0, 4, 5))


def local(valence_orbitals, conduction_orbitals, valence_energy, conduction_energy, grid_index):
    groups = tuple(lax.axis_size(name) for name in ("val", "cond", "grid"))
    val_groups, cond_groups, slabs = groups
    valence_local = valence_orbitals.shape[0]
    conduction_local = conduction_orbitals.shape[0]
    row_partials, column_partials = picked_partials(
        valence_orbitals, conduction_orbitals, grid_index, lax.axis_index("grid"), groups
    )
    rows = row_values(row_partials)
    columns = column_values(column_partials)
    delta = valence_energy[:, None] - conduction_energy[None, :]
    all_pairs = valence_energy.shape[0] * conduction_energy.shape[0]
    weights = 4.0 * delta / (delta * delta + freq_squared) / math.sqrt(all_pairs)
    weights = weights.reshape(val_groups, valence_local, cond_groups, conduction_local)
    weights = jnp.transpose(weights, (2, 0, 1, 3)).reshape(cond_groups, val_groups, 1, -1)
    weights = jnp.concatenate([weights, weights], axis=2)
    width = rows.shape[-1]
    split = (cond_groups, 2, val_groups // 2, slabs, rows.shape[2] // slabs)
    scaled = rows.reshape(split + (width,)).astype(jnp.float32) * weights.reshape(split + (1,))
    scaled = row_order(scaled.astype(jnp.bfloat16))
    swapped = jnp.concatenate([scaled[:, slabs // 2 :], -scaled[:, : slabs // 2]], axis=1)
    left = jnp.concatenate(
        [scaled.reshape(2 * all_pairs, width), swapped.reshape(2 * all_pairs, width)], axis=1
    )
    response = lax.dot_general(
        left, columns, (((0,), (0,)), ((), ())), preferred_element_type=jnp.float32
    )
    return response.reshape(2, width, columns.shape[1])


def solution(mesh):
    return jax.shard_map(
        local,
        mesh=mesh,
        in_specs=(P("val", "grid", None), P("cond", "grid", None), P(), P(), P()),
        out_specs=P(None, ("val", "grid"), "cond"),
        check_vma=False,
    )
```

```python
import math

import jax
import jax.numpy as jnp
import numpy as np
from jax import lax
from jax.experimental import pallas as pl
from jax.experimental.pallas import tpu as pltpu
from jax.sharding import PartitionSpec as P


NGRID = 96
NG = 6144
HALF = NGRID // 2 + 1
PITCH = 52
ROWS = 2 * PITCH
LANES = 128
ENTRY = 6
BLOCK = 128
GROUP = 4
FREQS = HALF + 1
YPAIRS = 5
FETCH = 4
SUB = 32

freq_squared = 4.0


def line_tables():
    indices = np.arange(NGRID)
    phases = indices[:, None] * indices[None, :] % NGRID
    angles = phases.astype(np.float32) * np.float32(2.0 * math.pi / NGRID)
    cos = np.cos(angles).astype(np.float32).astype(jnp.bfloat16)
    sin = (-np.sin(angles)).astype(np.float32).astype(jnp.bfloat16)
    return cos, sin


def z_matrix():
    cos, sin = line_tables()
    out = np.zeros((GROUP, ROWS, GROUP, NGRID), cos.dtype)
    for y in range(GROUP):
        out[y, :HALF, y] = cos[:HALF]
        out[y, PITCH : PITCH + HALF, y] = sin[:HALF]
    return out.reshape(GROUP * ROWS, GROUP * NGRID)


def y_matrix():
    cos, sin = line_tables()
    top = np.concatenate([cos.T, -(sin.T)], axis=1)
    bottom = np.concatenate([sin.T, cos.T], axis=1)
    return np.concatenate([top, bottom], axis=0)


def fold_matrix(tiles):
    out = np.zeros((tiles, SUB, SUB, 8), np.float32)
    for t in range(tiles):
        for j in range(SUB):
            out[t, j, j, t] = 1.0
            out[t, j, j, t + tiles] = 1.0
    return out.reshape(tiles * SUB, SUB * 8).astype(jnp.bfloat16)


def slab_matrix(pairs, depth):
    return np.kron(np.eye(pairs), np.ones((1, depth))).astype(jnp.bfloat16)


def tile_matrix(pairs, depth):
    return np.tile(np.eye(depth), (1, pairs)).astype(jnp.bfloat16)


def spectra_kernel(
    index_ref, val_ref, cond_ref, phase_ref, zmat_ref, ymat_ref, fold_ref, slab_ref,
    tile_ref, row_out, col_out, z_scr, table_scr, phase_scr, prod_a, prod_b, lines_a, lines_b,
    index_a, index_b, index_sem,
):
    index_scr = (index_a, index_b)
    bands_v, depth, points = val_ref.shape
    bands_c = cond_ref.shape[0]
    pairs = bands_v * bands_c
    width = pairs * depth
    tiles = width // LANES
    chunk = GROUP * NGRID

    def fetch(block, slot):
        pltpu.make_async_copy(
            index_ref.at[pl.ds(block * FETCH, FETCH)], index_scr[slot], index_sem.at[slot]
        ).start()

    fetch(0, 0)
    fetch(1, 1)

    wide = [
        jnp.dot(phase_ref[i], tile_ref[...], preferred_element_type=jnp.float32) for i in range(2)
    ]
    zeros = jnp.zeros((NGRID, LANES), jnp.float32)
    for sign in range(2):
        base = sign * NGRID * 16
        for s in range(8):
            t = s % tiles
            lanes = slice(t * LANES, (t + 1) * LANES)
            if s < tiles:
                first, second = wide[0][:, lanes], wide[1][:, lanes]
            elif s < 2 * tiles:
                first, second = -wide[1][:, lanes], wide[0][:, lanes]
            else:
                first, second = zeros, zeros
            if sign:
                second = -second
            phase_scr[pl.ds(base + s, NGRID, stride=16), :] = first
            phase_scr[pl.ds(base + 8 + s, NGRID, stride=16), :] = second
    table_scr[pl.ds(FREQS * NGRID * ENTRY, 8), :] = jnp.zeros((8, LANES), jnp.float32)

    def multiply(i, prod):
        for half in range(2):
            at = pl.multiple_of((2 * i + half) * chunk, LANES)
            cond = [cond_ref[c, :, pl.ds(at, chunk)].astype(jnp.float32) for c in range(bands_c)]
            for v in range(bands_v):
                orbital = val_ref[v, :, pl.ds(at, chunk)].astype(jnp.float32)
                rows = jnp.concatenate([orbital * cond[c] for c in range(bands_c)], axis=0)
                first = half * width + v * bands_c * depth
                prod[first : first + bands_c * depth, :] = rows.astype(jnp.bfloat16)

    def z_transform(i, prod):
        for y0, y1, k0, k1 in ((0, 2, 0, 256), (2, 3, 0, 384), (3, 4, 256, 384)):
            z_part = lax.dot_general(
                zmat_ref[y0 * ROWS : y1 * ROWS, k0:k1], prod[:, k0:k1],
                (((1,), (1,)), ((), ())), preferred_element_type=jnp.float32,
            )
            for half in range(2):
                row = pl.multiple_of(((2 * i + half) * GROUP + y0) * ROWS, 8)
                for t in range(tiles):
                    lane = half * width + t * LANES
                    z_scr[t, pl.ds(row, (y1 - y0) * ROWS), :] = z_part[:, lane : lane + LANES]

    z_last = points // (2 * chunk) - 1
    multiply(0, prod_a)

    def z_step(i, carry):
        z_transform(2 * i, prod_a)
        multiply(2 * i + 1, prod_b)
        z_transform(2 * i + 1, prod_b)
        multiply(jnp.minimum(2 * i + 2, z_last), prod_a)
        return carry

    lax.fori_loop(0, (z_last + 1) // 2, z_step, 0)

    def y_step(i, carry):
        for pair in range(YPAIRS):
            first = (i * YPAIRS + pair) * 2
            z_part = jnp.concatenate(
                [
                    jnp.concatenate(
                        [
                            z_scr[t, pl.ds(first + q + part * PITCH, NGRID, stride=ROWS), :]
                            for q in range(2)
                            for t in range(tiles)
                        ],
                        axis=1,
                    )
                    for part in range(2)
                ],
                axis=0,
            ).astype(jnp.bfloat16)
            plane = jnp.dot(ymat_ref[...], z_part, preferred_element_type=jnp.float32)
            for q in range(2):
                for part in range(2):
                    for t in range(tiles):
                        at = (first + q) * (NGRID * ENTRY) + part * tiles + t
                        lane = (q * tiles + t) * LANES
                        table_scr[pl.ds(at, NGRID, stride=ENTRY), :] = plane[
                            part * NGRID : (part + 1) * NGRID, lane : lane + LANES
                        ]
        return carry

    lax.fori_loop(0, FREQS // (2 * YPAIRS), y_step, 0)

    scale = NGRID ** (-1.5)

    def gather(slot, row, lines):
        for sub in range(BLOCK // SUB):
            real, imag = [], []
            for j in range(sub * SUB, (sub + 1) * SUB):
                entry = table_scr[pl.ds(index_scr[slot][row, 0, j], 8), :]
                line = pl.multiple_of(index_scr[slot][row, 1, j], 16)
                real.append(entry * phase_scr[pl.ds(line, 8), :])
                imag.append(entry * phase_scr[pl.ds(line + 8, 8), :])
            terms = jnp.concatenate(
                [jnp.concatenate(real, axis=0), jnp.concatenate(imag, axis=0)], axis=1
            ).astype(jnp.bfloat16)
            folded = jnp.dot(fold_ref[...], terms, preferred_element_type=jnp.float32)
            folded = folded.astype(jnp.bfloat16)
            for part in range(2):
                for t in range(tiles):
                    first = part * BLOCK + sub * SUB
                    lines[first : first + SUB, t * LANES : (t + 1) * LANES] = folded[
                        t * SUB : (t + 1) * SUB, part * LANES : (part + 1) * LANES
                    ]

    def add_x(block, lines):
        first = block * BLOCK
        row_block = first // row_out.shape[3]
        row_at = pl.multiple_of(first % row_out.shape[3], BLOCK)
        col_at = pl.multiple_of(first % col_out.shape[3], BLOCK)
        slabs, piece = col_out.shape[1:3]
        both = lax.dot_general(
            slab_ref[...], lines[...], (((1,), (1,)), ((), ())), preferred_element_type=jnp.float32
        )
        both = both * scale
        for part in range(2):
            value = both[:, part * BLOCK : (part + 1) * BLOCK]
            row_out[
                row_block % slabs, row_block // slabs, part * pairs : (part + 1) * pairs,
                pl.ds(row_at, BLOCK),
            ] = value.astype(row_out.dtype)
            for h in range(pairs // piece):
                col_out[
                    first // col_out.shape[3], part * (pairs // piece) + h, :, pl.ds(col_at, BLOCK)
                ] = value[h * piece : (h + 1) * piece].astype(col_out.dtype)

    def await_fetch(slot):
        pltpu.make_async_copy(
            index_ref.at[pl.ds(0, FETCH)], index_scr[slot], index_sem.at[slot]
        ).wait()

    last = NG // (BLOCK * FETCH) - 1
    await_fetch(0)
    gather(0, 0, lines_a)
    buffers = (lines_a, lines_b)

    def pick_step(i, carry):
        for n in range(2 * FETCH):
            slot, row = (n + 1) // FETCH % 2, (n + 1) % FETCH
            if row == 0:
                fetch(jnp.minimum(2 * i + n // FETCH + 2, last), 1 - slot)
                await_fetch(slot)
            gather(slot, row, buffers[(n + 1) % 2])
            add_x(2 * FETCH * i + n, buffers[n % 2])
        return carry

    lax.fori_loop(0, (last + 1) // 2, pick_step, 0)
    await_fetch(1)


def picked_partials(valence_orbitals, conduction_orbitals, grid_index, slab, groups):
    val_groups, cond_groups, slabs = groups
    bands_v, depth, _ = valence_orbitals.shape
    bands_c = conduction_orbitals.shape[0]
    pairs = bands_v * bands_c
    tiles = pairs * depth // LANES
    cos, sin = line_tables()
    phases = lax.dynamic_slice_in_dim(
        jnp.asarray(np.stack([cos.T, sin.T])), slab * depth, depth, 2
    )
    plane_size = NGRID * NGRID
    k = grid_index // plane_size
    p = grid_index // NGRID % NGRID
    q = grid_index % NGRID
    mirrored = q >= HALF
    k = jnp.where(mirrored, (NGRID - k) % NGRID, k)
    p = jnp.where(mirrored, (NGRID - p) % NGRID, p)
    q = jnp.where(mirrored, NGRID - q, q)
    rows = (q * NGRID + p) * ENTRY
    lines = (k + jnp.where(mirrored, NGRID, 0)) * 16
    constants = [
        jnp.asarray(a)
        for a in (
            z_matrix(), y_matrix(), fold_matrix(tiles), slab_matrix(pairs, depth),
            tile_matrix(pairs, depth),
        )
    ]
    index = jnp.stack([rows.reshape(-1, BLOCK), lines.reshape(-1, BLOCK)], axis=1)
    vmem = pl.BlockSpec(memory_space=pltpu.VMEM)
    return pl.pallas_call(
        spectra_kernel,
        out_shape=[
            jax.ShapeDtypeStruct(
                (slabs, val_groups, 2 * pairs, NG // (val_groups * slabs)), jnp.bfloat16
            ),
            jax.ShapeDtypeStruct(
                (cond_groups, slabs, 2 * pairs // slabs, NG // cond_groups), jnp.bfloat16
            ),
        ],
        in_specs=[pl.BlockSpec(memory_space=pl.ANY)] + [vmem] * (3 + len(constants)),
        out_specs=[vmem, vmem],
        scratch_shapes=[
            pltpu.VMEM((tiles, NGRID * ROWS, LANES), jnp.float32),
            pltpu.VMEM((FREQS * NGRID * ENTRY + 8, LANES), jnp.float32),
            pltpu.VMEM((2 * NGRID * 16, LANES), jnp.float32),
            pltpu.VMEM((2 * pairs * depth, GROUP * NGRID), jnp.bfloat16),
            pltpu.VMEM((2 * pairs * depth, GROUP * NGRID), jnp.bfloat16),
            pltpu.VMEM((2 * BLOCK, pairs * depth), jnp.bfloat16),
            pltpu.VMEM((2 * BLOCK, pairs * depth), jnp.bfloat16),
            pltpu.SMEM((FETCH, 2, BLOCK), jnp.int32),
            pltpu.SMEM((FETCH, 2, BLOCK), jnp.int32),
            pltpu.SemaphoreType.DMA((2,)),
        ],
        name="spectra",
    )(index, valence_orbitals, conduction_orbitals, phases, *constants)


def swap(value, axis, partner, first):
    count = lax.axis_size(axis)
    other = lax.ppermute(value, axis, [(i, partner(i)) for i in range(count)])
    return jnp.where(
        first, jnp.concatenate([value, other], 0), jnp.concatenate([other, value], 0)
    )


def row_values(partials):
    v, c, g = (lax.axis_index(name) for name in ("val", "cond", "grid"))
    slabs, groups, lines, width = partials.shape
    total = lax.dynamic_index_in_dim(partials, g, 0, keepdims=False).astype(jnp.float32)
    for step in range(1, slabs):
        piece = lax.dynamic_index_in_dim(partials, (g + step) % slabs, 0, keepdims=False)
        ring = [(i, (i + step) % slabs) for i in range(slabs)]
        other = lax.ppermute(piece, "grid", ring)
        total = total + other.astype(jnp.float32)
    total = total.astype(jnp.bfloat16)
    pieces = [lax.dynamic_index_in_dim(total, v, 0, keepdims=False)]
    for bits in range(1, groups):
        piece = lax.dynamic_index_in_dim(total, v ^ bits, 0, keepdims=False)
        pieces.append(lax.ppermute(piece, "val", [(i, i ^ bits) for i in range(groups)]))
    value = jnp.stack(pieces).reshape(2, 2, lines, width)
    value = jnp.where(v % 2 == 0, value, value[:, ::-1])
    value = jnp.where(v // 2 == 0, value, value[::-1])
    value = value.reshape(1, groups, lines, width)
    value = swap(value, "cond", lambda i: i ^ 1, c % 2 == 0)
    low, high, core = c // 2 % 2, c // 4, v % 2
    near, far = (lambda i: i ^ 2), (lambda i: (3 - i // 2) * 2 + i % 2)
    count = lax.axis_size("cond")

    def by_core(first, second):
        return [
            (i * count + j, i * count + (first if i % 2 == 0 else second)(j))
            for i in range(groups)
            for j in range(count)
        ]

    other = lax.ppermute(value, ("val", "cond"), by_core(near, far))
    first = jnp.where(core == 0, low, high) == 0
    own = jnp.where(first, jnp.stack([value, other]), jnp.stack([other, value]))
    other = lax.ppermute(own, ("val", "cond"), by_core(far, near))
    parts = []
    for h in range(2):
        for l in range(2):
            mine = jnp.where(core == 0, high == h, (low == l) == (high == h))
            if h == l:
                parts.append(jnp.where(mine, own[h], other[h]))
            else:
                by_low, by_high = jnp.where(mine, own[l], other[l]), jnp.where(mine, own[h], other[h])
                parts.append(jnp.where(core == 0, by_low, by_high))
    return jnp.stack(parts).reshape(count, groups, lines, width)


def column_values(partials):
    v, g = lax.axis_index("val"), lax.axis_index("grid")
    groups, slabs, piece, width = partials.shape
    received = lax.all_to_all(
        partials.reshape(groups * slabs, piece, width), ("cond", "grid"), 0, 0, tiled=True
    )
    value = jnp.sum(received.reshape(groups, slabs, piece, width).astype(jnp.float32), 1)
    value = value.astype(jnp.bfloat16).reshape(1, groups * piece, width)
    value = swap(value, "val", lambda i: i ^ 2, v // 2 == 0)
    value = swap(value, "grid", lambda i: i ^ 1, g % 2 == 0)
    value = swap(value, "grid", lambda i: 3 - i, g // 2 == 0)
    value = swap(value, "val", lambda i: i ^ 1, v % 2 == 0)
    return value.reshape(-1, width)


def row_order(value):
    return jnp.transpose(value, (2, 3, 1, 0, 4, 5))


def local(valence_orbitals, conduction_orbitals, valence_energy, conduction_energy, grid_index):
    groups = tuple(lax.axis_size(name) for name in ("val", "cond", "grid"))
    val_groups, cond_groups, slabs = groups
    valence_local = valence_orbitals.shape[0]
    conduction_local = conduction_orbitals.shape[0]
    row_partials, column_partials = picked_partials(
        valence_orbitals, conduction_orbitals, grid_index, lax.axis_index("grid"), groups
    )
    rows = row_values(row_partials)
    columns = column_values(column_partials)
    delta = valence_energy[:, None] - conduction_energy[None, :]
    all_pairs = valence_energy.shape[0] * conduction_energy.shape[0]
    weights = 4.0 * delta / (delta * delta + freq_squared) / math.sqrt(all_pairs)
    weights = weights.reshape(val_groups, valence_local, cond_groups, conduction_local)
    weights = jnp.transpose(weights, (2, 0, 1, 3)).reshape(cond_groups, val_groups, 1, -1)
    weights = jnp.concatenate([weights, weights], axis=2)
    width = rows.shape[-1]
    split = (cond_groups, 2, val_groups // 2, slabs, rows.shape[2] // slabs)
    scaled = rows.reshape(split + (width,)).astype(jnp.float32) * weights.reshape(split + (1,))
    scaled = row_order(scaled.astype(jnp.bfloat16))
    swapped = jnp.concatenate([scaled[:, slabs // 2 :], -scaled[:, : slabs // 2]], axis=1)
    left = jnp.concatenate(
        [scaled.reshape(2 * all_pairs, width), swapped.reshape(2 * all_pairs, width)], axis=1
    )
    response = lax.dot_general(
        left, columns, (((0,), (0,)), ((), ())), preferred_element_type=jnp.float32
    )
    return response.reshape(2, width, columns.shape[1])


def solution(mesh):
    return jax.shard_map(
        local,
        mesh=mesh,
        in_specs=(P("val", "grid", None), P("cond", "grid", None), P(), P(), P()),
        out_specs=P(None, ("val", "grid"), "cond"),
        check_vma=False,
    )
```
